256 devices in a mesh: grp: 8 (over y, core), mem: 32 (over x, z).
Axes of the slice: x: 4, y: 4, z: 8, core: 2. Of those that a mesh axis runs over, the one named last changes fastest.
Arguments:
- amplitudes: bfloat16 [8, 32, 384, 384], P('grp', 'mem'), may hold values from -6 to 6
- integrals: bfloat16 [8, 32, 384, 384], P('grp', 'mem'), may hold values from -0.3125 to 0.3125
- task_list: int32 [8, 2048, 3], P('grp'), may hold values from 0 to 31
- task_counts: int32 [8, 32], P('grp'), may hold values from 1 to 64, 1024 in all within a row
- owner_map: int32 [32], replicated, may hold values from 0 to 31, each once
Outputs:
- cycle: bfloat16 [8, 32, 384, 384], P('grp', 'mem')
The draws below stay inside these ranges and needn't reach their ends.
Inputs may be any that keep to these rules, and one draw needn't show every extreme that they name: `task_list`: rows 64 * e to 64 * (e + 1) - 1 of a group are executor e's task slots; every id is a tile id. `task_counts`: the counts of a group sum to 1024. `owner_map`: A permutation of the tile ids.
All inputs are finite; a program needn't handle non-finite values.
Results may differ from the reference program's by a relative error of at most 0.014.
Values may be sent and summed in bfloat16 or wider, within the bound.
No kernel may reach another device: no remote copies, remote signals or barrier semaphores. Data moves between devices by JAX's collectives and lax.ppermute only.
A program may use at most 192 MiB of HBM per device.

```python
import math
import jax
import jax.numpy as jnp
import numpy as np
from jax import lax

TILE = 384
TASK_DEV = 64
TILES = 32
LIVE_TOTAL = 1024
N_GRP = 8
N_MEM = 32


def set_ends(array, rng, low, high):
    shape = array.shape
    index_at = [jax.random.randint(jax.random.fold_in(rng, axis), (), 0, shape[axis]) for axis in range(len(shape))]
    array = array.at[tuple(index_at)].set(low)
    longest = shape.index(max(shape))
    index_at[longest] = (index_at[longest] + 1) % shape[longest]
    return array.at[tuple(index_at)].set(high)


def steps_of(stream_key, shape, cuts, low, high):
    def one(position, shards_of):
        steps = jax.random.uniform(jax.random.fold_in(jax.random.fold_in(stream_key, 6), position), (shards_of,), jnp.float32, low / len(cuts), high / len(cuts))
        return jnp.repeat(jnp.exp(steps), shape[position] // shards_of).reshape((-1,) + (1,) * (len(shape) - position - 1))

    level = one(*cuts[0])
    for cut in cuts[1:]:
        level = level * one(*cut)
    return level


def profile(number_of, total, reach, slope):
    weights = [(1 << 20) // math.isqrt(rank ** slope) + 1 for rank in range(2, number_of + 1)]
    rest, holding = total - reach - (number_of - 1), [1] * (number_of - 1)
    while rest > 0:
        free = [i for i in range(number_of - 1) if holding[i] < reach]
        pool, budget = sum([weights[i] for i in free]), rest
        for i in free:
            more = min(reach - holding[i], max(1, budget * weights[i] // pool), rest)
            holding[i] = holding[i] + more
            rest = rest - more
    return np.array([reach] + holding)


def ragged(stream_key, count, total, bound, slope):
    if count == 2:
        one = jax.random.randint(stream_key, (), max(1, total - bound), min(bound, total - 1) + 1)
        return jnp.stack([one, total - one])
    tallies = jnp.asarray(profile(count, total, bound, slope), jnp.int32)
    pairs = (count - 1) // 2
    donor, taker = tallies[1:1 + 2 * pairs:2], tallies[2:2 + 2 * pairs:2]
    margin = jnp.minimum(donor - 1, bound - taker)
    passed = jax.random.randint(jax.random.fold_in(stream_key, 1), (pairs,), 0, 1 << 20) % (margin + 1)
    tallies = tallies.at[1:1 + 2 * pairs:2].set(donor - passed).at[2:2 + 2 * pairs:2].set(taker + passed)
    return tallies[jax.random.permutation(jax.random.fold_in(stream_key, 2), count)]


def centred(stream_key, extent, spread, limit, pieces=(), held_as=jnp.bfloat16):
    drawn = spread * jax.random.normal(stream_key, extent, jnp.float32)
    if pieces:
        drawn = drawn * steps_of(stream_key, extent, pieces, -0.22, 0.18)
    return jnp.clip(drawn, -limit, limit).astype(held_as)


def setup_inputs(seed: int = 0) -> dict:
    key_of = jax.random.split(jax.random.key(seed), 6)
    amplitudes = centred(key_of[0], (N_GRP, TILES, TILE, TILE), 1.0, 6.0, ((0, 8), (1, 32)))
    integrals = centred(key_of[1], (N_GRP, TILES, TILE, TILE), TILE ** -0.5, 0.3125, ((0, 8), (1, 32)))
    task_list = set_ends(jax.random.randint(key_of[2], (N_GRP, N_MEM * TASK_DEV, 3), 0, TILES), jax.random.fold_in(key_of[2], 1), 0, TILES - 1).astype(jnp.int32)
    task_counts = jax.vmap(lambda own: ragged(own, N_MEM, LIVE_TOTAL, TASK_DEV, 2))(jax.random.split(key_of[3], N_GRP)).reshape((N_GRP, N_MEM)).astype(jnp.int32)
    owner_map = jax.random.permutation(key_of[4], TILES).astype(jnp.int32)
    return dict(amplitudes=amplitudes, integrals=integrals, task_list=task_list, task_counts=task_counts, owner_map=owner_map)


def reference(amplitudes, integrals, task_list, task_counts, owner_map):
    groups = N_GRP
    members = N_MEM
    amp_float = amplitudes.astype(jnp.float32)
    transposed = amp_float.reshape(groups, members, groups, TILE // groups, TILE)
    transposed = transposed.transpose(2, 1, 0, 3, 4).reshape(groups, members, TILE, TILE)
    mixed_tiles = (2.0 * amp_float - transposed).astype(jnp.bfloat16)
    holders = jnp.take(owner_map, task_list, axis=0).astype(jnp.int32)
    holder_grid = holders.reshape(groups, members, TASK_DEV, 3)
    live_all = jnp.arange(TASK_DEV, dtype=jnp.int32)[None, None, :] < task_counts[:, :, None]

    def one_group(inputs):
        group_mixed, group_int, group_holders, group_live = inputs

        def one_executor(running, inner):
            picked, living = inner
            left_tile = jnp.take(group_mixed, picked[:, 1], axis=0).astype(jnp.float32)
            right_tile = jnp.take(group_int, picked[:, 2], axis=0).astype(jnp.float32)
            product = jnp.einsum("kxy,kyz->kxz", left_tile, right_tile, precision=lax.Precision.HIGHEST)
            product = jnp.where(living[:, None, None], product, jnp.float32(0.0))
            partial_value = jnp.zeros((members, TILE, TILE), jnp.float32).at[picked[:, 0]].add(product)
            rounded = lax.optimization_barrier(partial_value.astype(jnp.bfloat16))
            return running + rounded.astype(jnp.float32), None

        start_sum = jnp.zeros((members, TILE, TILE), jnp.float32)
        running, _ = lax.scan(one_executor, start_sum, (group_holders, group_live))
        return running.astype(jnp.bfloat16)

    return lax.map(one_group, (mixed_tiles, integrals, holder_grid, live_all))
```

```python
import jax
import jax.numpy as jnp
from jax import lax
from jax.experimental import pallas as pl
from jax.experimental.pallas import tpu as pltpu
from jax.sharding import PartitionSpec as P

TILE = 384
TASK_DEV = 64
N_GRP = 8
N_MEM = 32
NX = 4
NZ = 8
RB = TILE // NZ

X_GROUPS = [[x * NZ + z for x in range(NX)] for z in range(NZ)]
Z_GROUPS = [[x * NZ + z for z in range(NZ)] for x in range(NX)]


def z_perm(step):
    return [(x * NZ + z, x * NZ + (z + step) % NZ) for x in range(NX) for z in range(NZ)]


def x_perm(step):
    return [(x * NZ + z, ((x + step) % NX) * NZ + z) for x in range(NX) for z in range(NZ)]


def contract_kernel(keys, starts, *refs):
    ints = refs[0:8]
    m0, m1, m2a, m2b, m3 = refs[8:13]
    out = refs[13]
    prod = refs[14]
    for b in range(8):
        right = ints[b][...]
        for base, left in ((0, m0), (8, m1), (16, m2a), (20, m2b), (24, m3)):
            rows = left.shape[0]
            got = jnp.dot(left[...], right, preferred_element_type=jnp.float32)
            prod[pl.ds(b * 32 + base, rows // RB)] = got.reshape(rows // RB, RB, TILE)

    def one_output(o, carry):
        def one_task(t, acc):
            return acc + prod[keys[t] & 255]

        acc = lax.fori_loop(starts[o], starts[o + 1], one_task, jnp.zeros((RB, TILE), jnp.float32))
        out[o] = acc.astype(jnp.bfloat16)
        return carry

    lax.fori_loop(0, N_MEM, one_output, 0)


def contract(keys, starts, ints, mixes):
    smem = pl.BlockSpec(memory_space=pltpu.SMEM)
    vmem = pl.BlockSpec(memory_space=pltpu.VMEM)
    return pl.pallas_call(
        contract_kernel,
        out_shape=jax.ShapeDtypeStruct((N_MEM, RB, TILE), jnp.bfloat16),
        in_specs=[smem, smem] + [vmem] * 13,
        out_specs=vmem,
        scratch_shapes=[pltpu.VMEM((8 * N_MEM, RB, TILE), jnp.float32)],
        compiler_params=pltpu.CompilerParams(vmem_limit_bytes=40 << 20),
    )(keys, starts, *ints, *mixes)


def task_keys(task_list, task_counts, owner_map, x, z):
    ids = jnp.arange(N_MEM, dtype=jnp.int32)
    hit = task_list[:, :, None] == ids[None, None, :]
    rows = jnp.sum(jnp.where(hit, owner_map[None, None, :], 0), axis=2)
    live = (jnp.arange(TASK_DEV, dtype=jnp.int32)[None, :] < task_counts[:, None]).reshape(-1)
    o, a, b = rows[:, 0], rows[:, 1], rows[:, 2]
    mine = live & ((b // NZ) == x)
    a_slot = ((a // NZ - x) % NX) * NZ + a % NZ
    b_slot = (b % NZ - z) % NZ
    key = jnp.where(mine, o * 256 + b_slot * 32 + a_slot, 1 << 20)
    keys = jnp.sort(key)
    edges = jnp.arange(N_MEM + 1, dtype=jnp.int32) * 256
    starts = jnp.sum((key[None, :] < edges[:, None]).astype(jnp.int32), axis=1)
    return keys, starts


def local(amplitudes, integrals, task_list, task_counts, owner_map):
    device = lax.axis_index("mem")
    x, z = device // NZ, device % NZ
    own_amp = amplitudes[0, 0]
    own_int = integrals[0, 0]

    ints = [None] * 8
    ints[0] = own_int
    fw = bw = own_int
    for step in range(1, 5):
        fw = lax.ppermute(fw, "mem", z_perm(1))
        ints[8 - step] = fw
        if step < 4:
            bw = lax.ppermute(bw, "mem", z_perm(-1))
            ints[step] = bw

    swapped = lax.all_to_all(own_amp, "grp", split_axis=0, concat_axis=0, tiled=True)
    mixed = (2.0 * own_amp.astype(jnp.float32) - swapped.astype(jnp.float32)).astype(jnp.bfloat16)
    m0 = lax.all_to_all(mixed, "mem", 0, 0, axis_index_groups=Z_GROUPS, tiled=True)
    m3 = lax.ppermute(m0, "mem", x_perm(1))
    m1 = lax.ppermute(m0, "mem", x_perm(-1))
    m2a = lax.ppermute(m3[: TILE // 2], "mem", x_perm(1))
    m2b = lax.ppermute(m1[TILE // 2 :], "mem", x_perm(-1))

    keys, starts = task_keys(task_list[0], task_counts[0], owner_map, x, z)
    part = contract(keys, starts, ints, (m0, m1, m2a, m2b, m3))
    got = lax.all_to_all(
        part.reshape(NX, NZ * RB, TILE), "mem", 0, 0, axis_index_groups=X_GROUPS, tiled=True
    )
    summed = jnp.sum(got.astype(jnp.float32), axis=0).astype(jnp.bfloat16)
    out = lax.all_to_all(summed, "mem", 0, 0, axis_index_groups=Z_GROUPS, tiled=True)
    return out[None, None]


def solution(mesh):
    placed = (
        P("grp", "mem", None, None),
        P("grp", "mem", None, None),
        P("grp", None, None),
        P("grp", None),
        P(),
    )
    return jax.shard_map(
        local, mesh=mesh, in_specs=placed, out_specs=P("grp", "mem", None, None), check_vma=False
    )
```

```python
import jax
import jax.numpy as jnp
from jax import lax
from jax.experimental import pallas as pl
from jax.experimental.pallas import tpu as pltpu
from jax.sharding import PartitionSpec as P


TILE = 384
TASK_DEV = 64
N_MEM = 32
NX = 4
NZ = 8
RB = TILE // NZ

X_GROUPS = [[x * NZ + z for x in range(NX)] for z in range(NZ)]
Z_GROUPS = [[x * NZ + z for z in range(NZ)] for x in range(NX)]


def z_perm(step):
    return [(x * NZ + z, x * NZ + (z + step) % NZ) for x in range(NX) for z in range(NZ)]


def x_perm(step):
    return [(x * NZ + z, ((x + step) % NX) * NZ + z) for x in range(NX) for z in range(NZ)]


FIRST = (0, 1, 2, 3, 5, 6, 7)


def sum_of(keys, source, first, last, acc, unroll):
    turns = (last - first) // unroll

    def some_tasks(turn, acc):
        for u in range(unroll):
            acc = acc + source[keys[first + turn * unroll + u] & 255]
        return acc

    def one_task(t, acc):
        return acc + source[keys[t] & 255]

    acc = lax.fori_loop(0, turns, some_tasks, acc)
    return lax.fori_loop(first + turns * unroll, last, one_task, acc)


def early_kernel(keys, starts, *refs):
    ints = refs[0:7]
    mixes = refs[7:10]
    sums, wide, prod = refs[10:13]
    for k in range(7):
        wide[:, k * TILE : (k + 1) * TILE] = ints[k][...]
    for k in (0, 2, 4, 6):
        span = min(2, 7 - k)
        right = wide[:, k * TILE : (k + span) * TILE]
        for m in range(3):
            got = jnp.dot(mixes[m][...], right, preferred_element_type=jnp.float32)
            for half in range(span):
                first = (k + half) * 3 * NZ + m * NZ
                block = got[:, half * TILE : (half + 1) * TILE]
                prod[first : first + NZ] = block.reshape(NZ, RB, TILE)

    def one_output(o, carry):
        acc = jnp.zeros((RB, TILE), jnp.float32)
        sums[o] = sum_of(keys, prod, starts[2 * o], starts[2 * o + 1], acc, 4)
        return carry

    lax.fori_loop(0, N_MEM, one_output, 0)


def early(keys, starts, ints, mixes):
    smem = pl.BlockSpec(memory_space=pltpu.SMEM)
    vmem = pl.BlockSpec(memory_space=pltpu.VMEM)
    return pl.pallas_call(
        early_kernel,
        out_shape=(
            jax.ShapeDtypeStruct((N_MEM, RB, TILE), jnp.float32),
            jax.ShapeDtypeStruct((TILE, 7 * TILE), jnp.bfloat16),
        ),
        in_specs=[smem, smem] + [vmem] * 10,
        out_specs=(vmem, vmem),
        scratch_shapes=[pltpu.VMEM((7 * 3 * NZ, RB, TILE), jnp.float32)],
        compiler_params=pltpu.CompilerParams(vmem_limit_bytes=30 << 20),
    )(keys, starts, *ints, *mixes)


def late_kernel(keys, starts, last_tile, m0, m1, m2, m3, sums, wide, out, rest):
    for m, left in enumerate((m0, m1, m3, m2)):
        got = jnp.dot(left[...], last_tile[...], preferred_element_type=jnp.float32)
        rest[(7 + m) * NZ : (8 + m) * NZ] = got.reshape(NZ, RB, TILE)
    for k in (0, 2, 4, 6):
        span = min(2, 7 - k)
        right = wide[:, k * TILE : (k + span) * TILE]
        got = jnp.dot(m2[...], right, preferred_element_type=jnp.float32)
        for half in range(span):
            block = got[:, half * TILE : (half + 1) * TILE]
            rest[(k + half) * NZ : (k + half + 1) * NZ] = block.reshape(NZ, RB, TILE)

    def one_output(o, carry):
        acc = sum_of(keys, rest, starts[2 * o + 1], starts[2 * o + 2], sums[o], 2)
        out[o] = acc.astype(jnp.bfloat16)
        return carry

    lax.fori_loop(0, N_MEM, one_output, 0)


def late(keys, starts, last_tile, mixes, sums, wide):
    smem = pl.BlockSpec(memory_space=pltpu.SMEM)
    vmem = pl.BlockSpec(memory_space=pltpu.VMEM)
    return pl.pallas_call(
        late_kernel,
        out_shape=jax.ShapeDtypeStruct((N_MEM, RB, TILE), jnp.bfloat16),
        in_specs=[smem, smem] + [vmem] * 7,
        out_specs=vmem,
        scratch_shapes=[pltpu.VMEM((11 * NZ, RB, TILE), jnp.float32)],
        compiler_params=pltpu.CompilerParams(vmem_limit_bytes=24 << 20),
    )(keys, starts, last_tile, *mixes, sums, wide)


def task_keys(task_list, task_counts, owner_map, x, z):
    ids = jnp.arange(N_MEM, dtype=jnp.int32)
    hit = task_list[:, :, None] == ids[None, None, :]
    rows = jnp.sum(jnp.where(hit, owner_map[None, None, :], 0), axis=2)
    live = (jnp.arange(TASK_DEV, dtype=jnp.int32)[None, :] < task_counts[:, None]).reshape(-1)
    o, a, b = rows[:, 0], rows[:, 1], rows[:, 2]
    mine = live & ((b // NZ) == x)
    a_turn, a_row = (a // NZ - x) % NX, a % NZ
    b_slot = (b % NZ - z) % NZ
    b_rank = jnp.where(b_slot > 4, b_slot - 1, b_slot)
    a_rank = jnp.where(a_turn == 3, 2, a_turn)
    in_early = (b_slot != 4) & (a_turn != 2)
    early_at = (b_rank * 3 + a_rank) * NZ + a_row
    last_at = (7 + jnp.where(a_turn == 2, 3, a_rank)) * NZ + a_row
    late_at = 256 + jnp.where(b_slot == 4, last_at, b_rank * NZ + a_row)
    key = jnp.where(mine, o * 512 + jnp.where(in_early, early_at, late_at), 1 << 20)
    keys = lax.sort(key, is_stable=False)
    edges = jnp.arange(2 * N_MEM + 1, dtype=jnp.int32) * 256
    starts = jnp.sum((key[None, :] < edges[:, None]).astype(jnp.int32), axis=1)
    return keys, starts


def local(amplitudes, integrals, task_list, task_counts, owner_map):
    device = lax.axis_index("mem")
    x, z = device // NZ, device % NZ
    own_amp = amplitudes[0, 0]
    own_int = integrals[0, 0]

    ints = [None] * 8
    ints[0] = own_int
    fw = bw = own_int
    for step in range(1, 5):
        fw = lax.ppermute(fw, "mem", z_perm(1))
        ints[8 - step] = fw
        if step < 4:
            bw = lax.ppermute(bw, "mem", z_perm(-1))
            ints[step] = bw

    swapped = lax.all_to_all(own_amp, "grp", split_axis=0, concat_axis=0, tiled=True)
    mixed = (2.0 * own_amp.astype(jnp.float32) - swapped.astype(jnp.float32)).astype(jnp.bfloat16)
    m0 = lax.all_to_all(mixed, "mem", 0, 0, axis_index_groups=Z_GROUPS, tiled=True)
    m3 = lax.ppermute(m0, "mem", x_perm(1))
    m1 = lax.ppermute(m0, "mem", x_perm(-1))
    m2 = lax.ppermute(m3, "mem", x_perm(1))

    keys, starts = task_keys(task_list[0], task_counts[0], owner_map, x, z)
    sums, wide = early(keys, starts, [ints[slot] for slot in FIRST], (m0, m1, m3))
    part = late(keys, starts, ints[4], (m0, m1, m2, m3), sums, wide)
    got = lax.all_to_all(
        part.reshape(NX, NZ * RB, TILE), "mem", 0, 0, axis_index_groups=X_GROUPS, tiled=True
    )
    summed = jnp.sum(got.astype(jnp.float32), axis=0).astype(jnp.bfloat16)
    out = lax.all_to_all(summed, "mem", 0, 0, axis_index_groups=Z_GROUPS, tiled=True)
    return out[None, None]


def solution(mesh):
    placed = (
        P("grp", "mem", None, None),
        P("grp", "mem", None, None),
        P("grp", None, None),
        P("grp", None),
        P(),
    )
    return jax.shard_map(
        local, mesh=mesh, in_specs=placed, out_specs=P("grp", "mem", None, None), check_vma=False
    )
```

```python
import jax
import jax.numpy as jnp
from jax import lax
from jax.experimental import pallas as pl
from jax.experimental.pallas import tpu as pltpu
from jax.sharding import PartitionSpec as P


TILE = 384
TASK_DEV = 64
N_MEM = 32
NX = 4
NZ = 8
RB = TILE // NZ

X_GROUPS = [[x * NZ + z for x in range(NX)] for z in range(NZ)]
Z_GROUPS = [[x * NZ + z for z in range(NZ)] for x in range(NX)]


def z_perm(step):
    return [(x * NZ + z, x * NZ + (z + step) % NZ) for x in range(NX) for z in range(NZ)]


def x_perm(step):
    return [(x * NZ + z, ((x + step) % NX) * NZ + z) for x in range(NX) for z in range(NZ)]


FIRST = (0, 1, 2, 3, 5, 6, 7)


def sum_of(keys, source, first, last, acc, unroll):
    turns = (last - first) // unroll

    def some_tasks(turn, acc):
        for u in range(unroll):
            acc = acc + source[keys[first + turn * unroll + u] & 255]
        return acc

    def one_task(t, acc):
        return acc + source[keys[t] & 255]

    acc = lax.fori_loop(0, turns, some_tasks, acc)
    return lax.fori_loop(first + turns * unroll, last, one_task, acc)


def early_kernel(keys, starts, *refs):
    ints = refs[0:7]
    mixes = refs[7:10]
    sums, wide, prod = refs[10:13]
    for k in range(7):
        wide[:, k * TILE : (k + 1) * TILE] = ints[k][...]
    for k in (0, 2, 4, 6):
        span = min(2, 7 - k)
        right = wide[:, k * TILE : (k + span) * TILE]
        for m in range(3):
            got = jnp.dot(mixes[m][...], right, preferred_element_type=jnp.float32)
            for half in range(span):
                first = (k + half) * 3 * NZ + m * NZ
                block = got[:, half * TILE : (half + 1) * TILE]
                prod[first : first + NZ] = block.reshape(NZ, RB, TILE)

    def one_output(o, carry):
        acc = jnp.zeros((RB, TILE), jnp.float32)
        sums[o] = sum_of(keys, prod, starts[2 * o], starts[2 * o + 1], acc, 4)
        return carry

    lax.fori_loop(0, N_MEM, one_output, 0)


def early(keys, starts, ints, mixes):
    smem = pl.BlockSpec(memory_space=pltpu.SMEM)
    vmem = pl.BlockSpec(memory_space=pltpu.VMEM)
    return pl.pallas_call(
        early_kernel,
        out_shape=(
            jax.ShapeDtypeStruct((N_MEM, RB, TILE), jnp.float32),
            jax.ShapeDtypeStruct((TILE, 7 * TILE), jnp.bfloat16),
        ),
        in_specs=[smem, smem] + [vmem] * 10,
        out_specs=(vmem, vmem),
        scratch_shapes=[pltpu.VMEM((7 * 3 * NZ, RB, TILE), jnp.float32)],
        compiler_params=pltpu.CompilerParams(vmem_limit_bytes=30 << 20),
    )(keys, starts, *ints, *mixes)


def late_kernel(keys, starts, last_tile, m0, m1, m2, m3, sums, wide, out, rest):
    for m, left in enumerate((m0, m1, m3, m2)):
        got = jnp.dot(left[...], last_tile[...], preferred_element_type=jnp.float32)
        rest[(7 + m) * NZ : (8 + m) * NZ] = got.reshape(NZ, RB, TILE)
    for k in (0, 2, 4, 6):
        span = min(2, 7 - k)
        right = wide[:, k * TILE : (k + span) * TILE]
        got = jnp.dot(m2[...], right, preferred_element_type=jnp.float32)
        for half in range(span):
            block = got[:, half * TILE : (half + 1) * TILE]
            rest[(k + half) * NZ : (k + half + 1) * NZ] = block.reshape(NZ, RB, TILE)

    def one_output(o, carry):
        acc = lax.fori_loop(
            starts[2 * o + 1],
            starts[2 * o + 2],
            lambda t, acc: acc + rest[keys[t] & 255],
            sums[o],
        )
        out[o] = acc.astype(jnp.bfloat16)
        return carry

    lax.fori_loop(0, N_MEM, one_output, 0)


def late(keys, starts, last_tile, mixes, sums, wide):
    smem = pl.BlockSpec(memory_space=pltpu.SMEM)
    vmem = pl.BlockSpec(memory_space=pltpu.VMEM)
    return pl.pallas_call(
        late_kernel,
        out_shape=jax.ShapeDtypeStruct((N_MEM, RB, TILE), jnp.bfloat16),
        in_specs=[smem, smem] + [vmem] * 7,
        out_specs=vmem,
        scratch_shapes=[pltpu.VMEM((11 * NZ, RB, TILE), jnp.float32)],
        compiler_params=pltpu.CompilerParams(vmem_limit_bytes=24 << 20),
    )(keys, starts, last_tile, *mixes, sums, wide)


def task_keys(task_list, task_counts, owner_map, x, z):
    ids = jnp.arange(N_MEM, dtype=jnp.int32)
    hit = task_list[:, :, None] == ids[None, None, :]
    rows = jnp.sum(jnp.where(hit, owner_map[None, None, :], 0), axis=2)
    live = (jnp.arange(TASK_DEV, dtype=jnp.int32)[None, :] < task_counts[:, None]).reshape(-1)
    o, a, b = rows[:, 0], rows[:, 1], rows[:, 2]
    mine = live & ((b // NZ) == x)
    a_turn, a_row = (a // NZ - x) % NX, a % NZ
    b_slot = (b % NZ - z) % NZ
    b_rank = jnp.where(b_slot > 4, b_slot - 1, b_slot)
    a_rank = jnp.where(a_turn == 3, 2, a_turn)
    in_early = (b_slot != 4) & (a_turn != 2)
    early_at = (b_rank * 3 + a_rank) * NZ + a_row
    last_at = (7 + jnp.where(a_turn == 2, 3, a_rank)) * NZ + a_row
    late_at = 256 + jnp.where(b_slot == 4, last_at, b_rank * NZ + a_row)
    key = jnp.where(mine, o * 512 + jnp.where(in_early, early_at, late_at), 1 << 20)
    keys = lax.sort(key, is_stable=False)
    edges = jnp.arange(2 * N_MEM + 1, dtype=jnp.int32) * 256
    starts = jnp.sum((key[None, :] < edges[:, None]).astype(jnp.int32), axis=1)
    return keys, starts


def local(amplitudes, integrals, task_list, task_counts, owner_map):
    device = lax.axis_index("mem")
    x, z = device // NZ, device % NZ
    own_amp = amplitudes[0, 0]
    own_int = integrals[0, 0]

    ints = [None] * 8
    ints[0] = own_int
    fw = bw = own_int
    for step in range(1, 5):
        fw = lax.ppermute(fw, "mem", z_perm(1))
        ints[8 - step] = fw
        if step < 4:
            bw = lax.ppermute(bw, "mem", z_perm(-1))
            ints[step] = bw

    doubled = lax.optimization_barrier(2.0 * own_amp.astype(jnp.float32))
    swapped = lax.all_to_all(own_amp, "grp", split_axis=0, concat_axis=0, tiled=True)
    mixed = (doubled - swapped.astype(jnp.float32)).astype(jnp.bfloat16)
    m0 = lax.all_to_all(mixed, "mem", 0, 0, axis_index_groups=Z_GROUPS, tiled=True)
    m3 = lax.ppermute(m0, "mem", x_perm(1))
    m1 = lax.ppermute(m0, "mem", x_perm(-1))
    m2 = lax.ppermute(m3, "mem", x_perm(1))

    keys, starts = task_keys(task_list[0], task_counts[0], owner_map, x, z)
    sums, wide = early(keys, starts, [ints[slot] for slot in FIRST], (m0, m1, m3))
    part = late(keys, starts, ints[4], (m0, m1, m2, m3), sums, wide)
    got = lax.all_to_all(
        part.reshape(NX, NZ * RB, TILE), "mem", 0, 0, axis_index_groups=X_GROUPS, tiled=True
    )
    summed = jnp.sum(got.astype(jnp.float32), axis=0).astype(jnp.bfloat16)
    out = lax.all_to_all(summed, "mem", 0, 0, axis_index_groups=Z_GROUPS, tiled=True)
    return out[None, None]


def solution(mesh):
    placed = (
        P("grp", "mem", None, None),
        P("grp", "mem", None, None),
        P("grp", None, None),
        P("grp", None),
        P(),
    )
    return jax.shard_map(
        local, mesh=mesh, in_specs=placed, out_specs=P("grp", "mem", None, None), check_vma=False
    )
```

```python
import jax
import jax.numpy as jnp
from jax import lax
from jax.experimental import pallas as pl
from jax.experimental.pallas import tpu as pltpu
from jax.sharding import PartitionSpec as P


TILE = 384
TASK_DEV = 64
N_MEM = 32
NX = 4
NZ = 8
RB = TILE // NZ

X_GROUPS = [[x * NZ + z for x in range(NX)] for z in range(NZ)]
Z_GROUPS = [[x * NZ + z for z in range(NZ)] for x in range(NX)]


def z_perm(step):
    return [(x * NZ + z, x * NZ + (z + step) % NZ) for x in range(NX) for z in range(NZ)]


def x_perm(step):
    return [(x * NZ + z, ((x + step) % NX) * NZ + z) for x in range(NX) for z in range(NZ)]


FIRST = (0, 1, 2, 3, 5, 6, 7)


def sum_of(keys, source, first, last, acc, unroll):
    turns = (last - first) // unroll

    def some_tasks(turn, acc):
        for u in range(unroll):
            acc = acc + source[keys[first + turn * unroll + u] & 255]
        return acc

    def one_task(t, acc):
        return acc + source[keys[t] & 255]

    acc = lax.fori_loop(0, turns, some_tasks, acc)
    return lax.fori_loop(first + turns * unroll, last, one_task, acc)


def early_kernel(keys, starts, *refs):
    ints = refs[0:7]
    mixes = refs[7:10]
    sums, wide, prod = refs[10:13]
    for k in range(7):
        wide[:, k * TILE : (k + 1) * TILE] = ints[k][...]
    for k in (0, 2, 4, 6):
        span = min(2, 7 - k)
        right = wide[:, k * TILE : (k + span) * TILE]
        for m in range(3):
            got = jnp.dot(mixes[m][...], right, preferred_element_type=jnp.float32)
            for half in range(span):
                first = (k + half) * 3 * NZ + m * NZ
                block = got[:, half * TILE : (half + 1) * TILE]
                prod[first : first + NZ] = block.reshape(NZ, RB, TILE)

    def one_output(o, carry):
        acc = jnp.zeros((RB, TILE), jnp.float32)
        sums[o] = sum_of(keys, prod, starts[2 * o], starts[2 * o + 1], acc, 4)
        return carry

    lax.fori_loop(0, N_MEM, one_output, 0)


def early(keys, starts, ints, mixes):
    smem = pl.BlockSpec(memory_space=pltpu.SMEM)
    vmem = pl.BlockSpec(memory_space=pltpu.VMEM)
    return pl.pallas_call(
        early_kernel,
        out_shape=(
            jax.ShapeDtypeStruct((N_MEM, RB, TILE), jnp.float32),
            jax.ShapeDtypeStruct((TILE, 7 * TILE), jnp.bfloat16),
        ),
        in_specs=[smem, smem] + [vmem] * 10,
        out_specs=(vmem, vmem),
        scratch_shapes=[pltpu.VMEM((7 * 3 * NZ, RB, TILE), jnp.float32)],
        compiler_params=pltpu.CompilerParams(vmem_limit_bytes=30 << 20),
    )(keys, starts, *ints, *mixes)


def late_kernel(keys, starts, last_tile, m0, m1, m2, m3, sums, wide, out, rest):
    for m, left in enumerate((m0, m1, m3, m2)):
        got = jnp.dot(left[...], last_tile[...], preferred_element_type=jnp.float32)
        rest[(7 + m) * NZ : (8 + m) * NZ] = got.reshape(NZ, RB, TILE)
    for k in (0, 2, 4, 6):
        span = min(2, 7 - k)
        right = wide[:, k * TILE : (k + span) * TILE]
        got = jnp.dot(m2[...], right, preferred_element_type=jnp.float32)
        for half in range(span):
            block = got[:, half * TILE : (half + 1) * TILE]
            rest[(k + half) * NZ : (k + half + 1) * NZ] = block.reshape(NZ, RB, TILE)

    def one_output(o, carry):
        acc = lax.fori_loop(
            starts[2 * o + 1],
            starts[2 * o + 2],
            lambda t, acc: acc + rest[keys[t] & 255],
            sums[o],
        )
        out[o] = acc.astype(jnp.bfloat16)
        return carry

    lax.fori_loop(0, N_MEM, one_output, 0)


def late(keys, starts, last_tile, mixes, sums, wide):
    smem = pl.BlockSpec(memory_space=pltpu.SMEM)
    vmem = pl.BlockSpec(memory_space=pltpu.VMEM)
    return pl.pallas_call(
        late_kernel,
        out_shape=jax.ShapeDtypeStruct((N_MEM, RB, TILE), jnp.bfloat16),
        in_specs=[smem, smem] + [vmem] * 7,
        out_specs=vmem,
        scratch_shapes=[pltpu.VMEM((11 * NZ, RB, TILE), jnp.float32)],
        compiler_params=pltpu.CompilerParams(vmem_limit_bytes=24 << 20),
    )(keys, starts, last_tile, *mixes, sums, wide)


def task_keys(task_list, task_counts, owner_map, x, z):
    ids = jnp.arange(N_MEM, dtype=jnp.int32)
    hit = task_list[:, :, None] == ids[None, None, :]
    rows = jnp.sum(jnp.where(hit, owner_map[None, None, :], 0), axis=2)
    live = (jnp.arange(TASK_DEV, dtype=jnp.int32)[None, :] < task_counts[:, None]).reshape(-1)
    o, a, b = rows[:, 0], rows[:, 1], rows[:, 2]
    mine = live & ((b // NZ) == x)
    a_turn, a_row = (a // NZ - x) % NX, a % NZ
    b_slot = (b % NZ - z) % NZ
    b_rank = jnp.where(b_slot > 4, b_slot - 1, b_slot)
    a_rank = jnp.where(a_turn == 3, 2, a_turn)
    in_early = (b_slot != 4) & (a_turn != 2)
    early_at = (b_rank * 3 + a_rank) * NZ + a_row
    last_at = (7 + jnp.where(a_turn == 2, 3, a_rank)) * NZ + a_row
    late_at = 256 + jnp.where(b_slot == 4, last_at, b_rank * NZ + a_row)
    key = jnp.where(mine, o * 512 + jnp.where(in_early, early_at, late_at), 1 << 20)
    keys = lax.sort(key, is_stable=False)
    edges = jnp.arange(2 * N_MEM + 1, dtype=jnp.int32) * 256
    starts = jnp.sum((key[None, :] < edges[:, None]).astype(jnp.int32), axis=1)
    return keys, starts


def local(amplitudes, integrals, task_list, task_counts, owner_map):
    device = lax.axis_index("mem")
    x, z = device // NZ, device % NZ
    own_amp = amplitudes[0, 0]
    own_int = integrals[0, 0]

    ints = [None] * 8
    ints[0] = own_int
    fw = bw = own_int
    for step in range(1, 5):
        fw = lax.ppermute(fw, "mem", z_perm(-1))
        ints[step] = fw
        if step < 4:
            bw = lax.ppermute(bw, "mem", z_perm(1))
            ints[8 - step] = bw

    doubled = lax.optimization_barrier(2.0 * own_amp.astype(jnp.float32))
    swapped = lax.all_to_all(own_amp, "grp", split_axis=0, concat_axis=0, tiled=True)
    mixed = (doubled - swapped.astype(jnp.float32)).astype(jnp.bfloat16)
    m0 = lax.all_to_all(mixed, "mem", 0, 0, axis_index_groups=Z_GROUPS, tiled=True)
    m3 = lax.ppermute(m0, "mem", x_perm(1))
    m1 = lax.ppermute(m0, "mem", x_perm(-1))
    m2 = lax.ppermute(m3, "mem", x_perm(1))

    keys, starts = task_keys(task_list[0], task_counts[0], owner_map, x, z)
    sums, wide = early(keys, starts, [ints[slot] for slot in FIRST], (m0, m1, m3))
    part = late(keys, starts, ints[4], (m0, m1, m2, m3), sums, wide)
    got = lax.all_to_all(
        part.reshape(NX, NZ * RB, TILE), "mem", 0, 0, axis_index_groups=X_GROUPS, tiled=True
    )
    summed = jnp.sum(got.astype(jnp.float32), axis=0).astype(jnp.bfloat16)
    out = lax.all_to_all(summed, "mem", 0, 0, axis_index_groups=Z_GROUPS, tiled=True)
    return out[None, None]


def solution(mesh):
    placed = (
        P("grp", "mem", None, None),
        P("grp", "mem", None, None),
        P("grp", None, None),
        P("grp", None),
        P(),
    )
    return jax.shard_map(
        local, mesh=mesh, in_specs=placed, out_specs=P("grp", "mem", None, None), check_vma=False
    )
```
